256 devices in a mesh: chan: 64 (over y, x, z_lo), tm: 4 (over z_hi, core).
Axes of the slice: x: 4, y: 4, z: 8 (z_hi: 2, z_lo: 4; z = z_hi * 4 + z_lo), core: 2. Of those that a mesh axis runs over, the one named last changes fastest.
Arguments:
- samples: int32 [256, 1048576], P('chan', 'tm'), may hold values from -8 to 7
Outputs:
- visibilities: float32 [1024, 2, 256, 256], P(('chan', 'tm'))
The draws below stay inside these ranges and needn't reach their ends.
All inputs are finite; a program needn't handle non-finite values.
Results may differ from the reference program's by a relative error of at most 0.00055.
Values may be sent and summed in bfloat16 or wider, within the bound.
A program may use at most 128 MiB of HBM per device.

```python
import jax
import jax.numpy as jnp
from jax import lax

INPUTS = 256
CH = 1024
TAPS = 16
LEN = 2048
SPEC = 512


def with_ends(values, own_key, low, high):
    longest = values.shape.index(max(values.shape))
    spots = []
    for shift in (0, 1):
        where = [jax.random.randint(jax.random.fold_in(own_key, axis), (), 0, length) for axis, length in enumerate(values.shape)]
        where[longest] = (where[longest] + shift) % values.shape[longest]
        spots.append(tuple(where))
    return values.at[spots[0]].set(low).at[spots[1]].set(high)


def setup_inputs(seed: int = 0) -> dict:
    seeds = jax.random.split(jax.random.key(seed), 2)
    return {
        "samples": with_ends(jax.random.randint(seeds[0], (INPUTS, SPEC * LEN), -8, 8), jax.random.fold_in(seeds[0], 1), -8, 7).astype(jnp.int32),
    }


NOISE_POWER = 21.25

def filter_taps(frame_len, tap_count):
    tap_index = jnp.arange(tap_count, dtype=jnp.int32)[:, None]
    sample_index = jnp.arange(frame_len, dtype=jnp.int32)[None, :]
    position = (tap_count - 1 - tap_index) * frame_len + sample_index
    where_at = position.astype(jnp.float32)
    argument = (where_at - jnp.float32(tap_count * frame_len / 2)) / jnp.float32(frame_len)
    window = 0.5 - 0.5 * jnp.cos(2.0 * jnp.pi * where_at / jnp.float32(tap_count * frame_len))
    return (jnp.sinc(argument) * window).astype(jnp.float32)

def reference(samples):
    weights = filter_taps(LEN, TAPS)
    frames = samples.reshape(INPUTS, SPEC, LEN)

    def one_input(frames_one):
        values = frames_one.astype(jnp.float32)
        padded = jnp.pad(values, ((TAPS - 1, 0), (0, 0)))
        filtered = jnp.zeros((SPEC, LEN), jnp.float32)
        for tap_index in range(TAPS):
            lead = TAPS - 1 - tap_index
            filtered = filtered + weights[tap_index][None, :] * padded[lead:lead + SPEC]
        transform = jnp.fft.rfft(filtered, axis=1)[:, :CH] / jnp.sqrt(jnp.float32(LEN))
        parts = jnp.stack([jnp.real(transform), jnp.imag(transform)], axis=2)
        return parts.astype(jnp.float32).astype(jnp.bfloat16)
    spectra = lax.map(one_input, frames)
    arranged = jnp.transpose(spectra, (2, 3, 0, 1))
    vis_scale = jnp.float32(1.0 / (NOISE_POWER * SPEC))

    def one_channel(chan_block):
        stacked = chan_block.reshape(2 * INPUTS, SPEC).astype(jnp.float32)
        gram_all = jnp.dot(stacked, stacked.T, preferred_element_type=jnp.float32, precision=lax.Precision.HIGHEST)
        real_vis = gram_all[:INPUTS, :INPUTS] + gram_all[INPUTS:, INPUTS:]
        imag_vis = gram_all[INPUTS:, :INPUTS] - gram_all[:INPUTS, INPUTS:]
        return jnp.stack([real_vis, imag_vis], axis=0) * vis_scale
    return lax.map(one_channel, arranged)
```

```python
import functools

import jax
import jax.numpy as jnp
from jax import lax
from jax.experimental import pallas as pl
from jax.experimental.pallas import tpu as pltpu
from jax.sharding import PartitionSpec as P

CH = 1024
TAPS = 16
NOISE_POWER = 21.25
MESH = pl.DeviceIdType.MESH


def filter_taps(frame_len, tap_count):
    tap_index = jnp.arange(tap_count, dtype=jnp.int32)[:, None]
    sample_index = jnp.arange(frame_len, dtype=jnp.int32)[None, :]
    position = (tap_count - 1 - tap_index) * frame_len + sample_index
    where_at = position.astype(jnp.float32)
    argument = (where_at - jnp.float32(tap_count * frame_len / 2)) / jnp.float32(frame_len)
    window = 0.5 - 0.5 * jnp.cos(2.0 * jnp.pi * where_at / jnp.float32(tap_count * frame_len))
    return (jnp.sinc(argument) * window).astype(jnp.float32)


def fourier_table(frame_len, chan_total):
    sample_index = jnp.arange(frame_len, dtype=jnp.int32)[None, :]
    chan_index = jnp.arange(chan_total, dtype=jnp.int32)[:, None]
    phase_step = sample_index * chan_index % frame_len
    angle = 2.0 * jnp.pi * phase_step.astype(jnp.float32) / jnp.float32(frame_len)
    norm_factor = 1.0 / jnp.sqrt(jnp.float32(frame_len))
    parts = jnp.stack([jnp.cos(angle) * norm_factor, -jnp.sin(angle) * norm_factor], axis=1)
    return parts.reshape(2 * chan_total, frame_len)


def exchange_kernel(chans, times, sent_ref, got_ref, send_sem, recv_sem, own_sem):
    total = chans * times
    me = lax.axis_index("chan") * times + lax.axis_index("tm")
    barrier = pltpu.get_barrier_semaphore()

    def greet(step, _):
        peer = lax.rem(me + step, total)
        pl.semaphore_signal(
            barrier, inc=1, device_id=(peer // times, peer % times), device_id_type=MESH
        )
        return 0

    lax.fori_loop(1, total, greet, 0)
    pl.semaphore_wait(barrier, total - 1)
    own = pltpu.make_async_copy(sent_ref.at[me], got_ref.at[me], own_sem)
    own.start()

    def send(step, _):
        peer = lax.rem(me + step, total)
        pltpu.make_async_remote_copy(
            sent_ref.at[peer],
            got_ref.at[me],
            send_sem,
            recv_sem,
            device_id=(peer // times, peer % times),
            device_id_type=MESH,
        ).start()
        return 0

    lax.fori_loop(1, total, send, 0)
    own.wait()
    others = pl.ds(0, total - 1)
    pltpu.make_async_copy(sent_ref.at[others], sent_ref.at[others], send_sem).wait()
    pltpu.make_async_copy(got_ref.at[others], got_ref.at[others], recv_sem).wait()


def exchange(blocks, chans, times):
    return pl.pallas_call(
        functools.partial(exchange_kernel, chans, times),
        out_shape=jax.ShapeDtypeStruct(blocks.shape, blocks.dtype),
        in_specs=[pl.BlockSpec(memory_space=pltpu.VMEM)],
        out_specs=pl.BlockSpec(memory_space=pltpu.VMEM),
        scratch_shapes=[pltpu.SemaphoreType.DMA] * 3,
        compiler_params=pltpu.CompilerParams(
            collective_id=0, has_side_effects=True, vmem_limit_bytes=40 << 20
        ),
    )(blocks)


def body(samples):
    chans = lax.axis_size("chan")
    times = lax.axis_size("tm")
    frame_len = 2 * CH
    inp_dev = samples.shape[0]
    spec_dev = samples.shape[1] // frame_len
    frames = samples.reshape(inp_dev, spec_dev, frame_len).astype(jnp.bfloat16)
    halo = lax.ppermute(
        frames[:, spec_dev - (TAPS - 1) :], "tm", [(i, i + 1) for i in range(times - 1)]
    )
    padded = jnp.concatenate([halo, frames], axis=1)
    weights = filter_taps(frame_len, TAPS)
    filtered = jnp.zeros((inp_dev, spec_dev, frame_len), jnp.float32)
    for tap_index in range(TAPS):
        lead = TAPS - 1 - tap_index
        filtered = filtered + weights[tap_index][None, None, :] * padded[
            :, lead : lead + spec_dev
        ].astype(jnp.float32)
    table = fourier_table(frame_len, CH)
    spectra = jnp.einsum(
        "cn,isn->cis",
        table,
        filtered,
        preferred_element_type=jnp.float32,
        precision=lax.Precision.HIGH,
    )
    own_chans = CH // (chans * times)
    blocks = spectra.astype(jnp.bfloat16).reshape(chans * times, 2 * own_chans, inp_dev, spec_dev)
    got = exchange(blocks, chans, times)
    got = got.reshape(chans, times, own_chans, 2, inp_dev, spec_dev)
    parts = got.transpose(2, 0, 4, 3, 1, 5).reshape(own_chans, chans * inp_dev, 2, times * spec_dev)
    turned = jnp.stack([parts[:, :, 1], -parts[:, :, 0]], axis=2)
    vis_scale = jnp.float32(1.0 / (NOISE_POWER * spec_dev * times))
    real_vis = jnp.einsum("carn,cbrn->cab", parts, parts, preferred_element_type=jnp.float32)
    imag_vis = jnp.einsum("carn,cbrn->cab", turned, parts, preferred_element_type=jnp.float32)
    return jnp.stack([real_vis, imag_vis], axis=1) * vis_scale


def solution(mesh):
    return jax.shard_map(
        body,
        mesh=mesh,
        in_specs=(P("chan", "tm"),),
        out_specs=P(("chan", "tm"), None, None, None),
        check_vma=False,
    )
```

```python
import functools

import jax
import jax.numpy as jnp
import numpy as np
from jax import lax
from jax.experimental import pallas as pl
from jax.experimental.pallas import tpu as pltpu
from jax.sharding import PartitionSpec as P

CH = 1024
TAPS = 16
NOISE_POWER = 21.25
MESH = pl.DeviceIdType.MESH
LANES = 128
RADIX = 2 * CH // LANES
PAIRS = RADIX // 2
CONTRACT_LANES = (((1,), (1,)), ((), ()))


def filter_table(inputs):
    frame_len = 2 * CH
    position = (TAPS - 1 - np.arange(TAPS))[:, None] * frame_len + np.arange(frame_len)[None, :]
    argument = (position - TAPS * frame_len / 2) / frame_len
    window = 0.5 - 0.5 * np.cos(2.0 * np.pi * position / (TAPS * frame_len))
    weights = (np.sinc(argument) * window).astype(np.float32)
    weights = weights.reshape(TAPS, RADIX, 1, LANES)
    return np.broadcast_to(weights, (TAPS, RADIX, inputs, LANES)).reshape(TAPS, -1, LANES)


def fourier_tables():
    table = np.zeros((PAIRS, 2, 2, CH // RADIX, 2, LANES), np.float64)
    lane = np.arange(LANES)[None, :]
    for q in range(PAIRS):
        for side in range(2):
            residue = (q, RADIX - q if q else PAIRS)[side]
            chan = residue + RADIX * np.arange(CH // RADIX)[:, None]
            angle = 2.0 * np.pi * (chan * lane % (2 * CH)) / (2 * CH)
            cos, sin = np.cos(angle), np.sin(angle)
            if q == 0:
                table[q, side, 0, :, side] = cos
                table[q, side, 1, :, side] = -sin
            else:
                sign = (1, -1)[side]
                table[q, side, 0, :, 0] = cos
                table[q, side, 0, :, 1] = sign * sin
                table[q, side, 1, :, 0] = -sin
                table[q, side, 1, :, 1] = sign * cos
    table = (table / np.sqrt(2.0 * CH)).reshape(PAIRS, 2 * LANES, 2 * LANES).astype(np.float32)
    high = table.astype(jnp.bfloat16)
    low = (table - high.astype(np.float32)).astype(jnp.bfloat16)
    return high, low


def first_stage(x):
    a = [x[n] + x[n + 8] for n in range(8)]
    b = [x[n] - x[n + 8] for n in range(8)]
    out = [None] * 8
    aa = [a[n] + a[n + 4] for n in range(4)]
    ab = [a[n] - a[n + 4] for n in range(4)]
    even, odd = aa[0] + aa[2], aa[1] + aa[3]
    out[0] = (even + odd, even - odd)
    out[4] = (aa[0] - aa[2], aa[3] - aa[1])
    root = float(np.sqrt(0.5))
    plus, minus = (ab[1] + ab[3]) * root, (ab[1] - ab[3]) * root
    out[2] = (ab[0] + minus, -(ab[2] + plus))
    out[6] = (ab[0] - minus, ab[2] - plus)
    d = [b[n] - b[8 - n] for n in range(1, 4)]
    e = [b[n] + b[8 - n] for n in range(1, 4)]
    for k in (1, 3, 5, 7):
        re = b[0]
        im = -b[4] if k % 4 == 1 else b[4]
        for n in range(1, 4):
            re = re + d[n - 1] * float(np.cos(np.pi * k * n / 8))
            im = im - e[n - 1] * float(np.sin(np.pi * k * n / 8))
        out[k] = (re, im)
    return out


def spectra_kernel(
    chans, times, inputs, spec,
    x_hbm, w_ref, high_ref, low_ref, got_ref,
    x_buf, tail_buf, tail_out, halo, halo_wide, wide, y_high, y_low, sent,
    x_sem, tail_sem, halo_send, halo_recv, send_sem, recv_sem, own_sem, all_in,
):
    total = chans * times
    ahead = TAPS - 1
    rows = RADIX * inputs
    groups = rows // 8
    chan, tm = lax.axis_index("chan"), lax.axis_index("tm")
    barrier = pltpu.get_barrier_semaphore()

    tail_copy = pltpu.make_async_copy(x_hbm.at[pl.ds(spec - ahead, ahead)], tail_buf, tail_sem)
    tail_copy.start()

    def piece(g):
        part = pl.ds(pl.multiple_of(g * 8, 8), 8)
        return pltpu.make_async_copy(x_hbm.at[:, part], x_buf.at[:, part], x_sem.at[g])

    for g in range(groups):
        piece(g).start()

    line = chans // times
    row, column = chan // times, chan % times * times + tm

    def row_peer(step):
        at = lax.rem(column + step, line)
        return (row * times + at // times, at % times)

    def column_peer(step):
        return (lax.rem(row + step, line) * times + chan % times, tm)

    def signal(semaphore, peer):
        pl.semaphore_signal(semaphore, inc=1, device_id=peer, device_id_type=MESH)

    for step in range(1, line):
        signal(barrier, row_peer(step))
        signal(barrier, column_peer(step))

    tail_copy.wait()
    for f in range(ahead):
        tail_out[f] = tail_buf[f].astype(jnp.float32).astype(jnp.bfloat16)

    pl.semaphore_wait(barrier, 2 * (line - 1))
    for step in range(1, line):
        signal(all_in, column_peer(step))

    @pl.when(tm < times - 1)
    def _():
        pltpu.make_async_remote_copy(
            tail_out, halo, halo_send, halo_recv,
            device_id=(chan, lax.rem(tm + 1, times)), device_id_type=MESH,
        ).start()

    def filtered(taps, window, base, fresh, r0):
        seq = list(window) + fresh
        for j in range(TAPS):
            acc = taps[0] * seq[ahead + j]
            for p in range(1, TAPS):
                acc = acc + taps[p] * seq[ahead + j - p]
            wide[pl.ds(r0 * spec + base + j, 8, stride=spec), :] = acc
        return tuple(seq[TAPS:])

    def frame(s, r0):
        return x_buf[s, pl.ds(r0, 8), :].astype(jnp.float32)

    def tap_rows(r0):
        return [w_ref[p, pl.ds(r0, 8), :] for p in range(TAPS)]

    def own_frames(g, _):
        r0 = pl.multiple_of(g * 8, 8)
        piece(g).wait()
        taps = tap_rows(r0)
        window = tuple(frame(s, r0) for s in range(1, TAPS))

        def block(n, window):
            base = TAPS + n * TAPS
            fresh = [frame(base + j, r0) for j in range(TAPS)]
            return filtered(taps, window, base, fresh, r0)

        lax.fori_loop(0, spec // TAPS - 1, block, window)
        return 0

    lax.fori_loop(0, groups, own_frames, 0)

    @pl.when(tm > 0)
    def _():
        pltpu.make_async_copy(halo, halo, halo_recv).wait()
        for f in range(ahead):
            halo_wide[f] = halo[f].astype(jnp.float32)

    @pl.when(tm == 0)
    def _():
        for f in range(ahead):
            halo_wide[f] = jnp.zeros((rows, LANES), jnp.float32)

    def first_frames(g, _):
        r0 = pl.multiple_of(g * 8, 8)
        window = [halo_wide[f, pl.ds(r0, 8), :] for f in range(ahead)]
        filtered(tap_rows(r0), window, 0, [frame(j, r0) for j in range(TAPS)], r0)
        return 0

    lax.fori_loop(0, groups, first_frames, 0)

    def butterflies(n, _):
        i, s0 = n // (spec // 16), n % (spec // 16) * 16
        x = [
            wide[pl.ds(pl.multiple_of((row * inputs + i) * spec + s0, 16), 16), :]
            for row in range(RADIX)
        ]
        place = pl.ds(pl.multiple_of(i * spec + s0, 16), 16)
        for q, parts in enumerate(first_stage(x)):
            for part, value in enumerate(parts):
                lanes = pl.ds(part * LANES, LANES)
                high = value.astype(jnp.bfloat16)
                y_high[q, place, lanes] = high
                y_low[q, place, lanes] = (value - high.astype(jnp.float32)).astype(jnp.bfloat16)
        return 0

    lax.fori_loop(0, inputs * spec // 16, butterflies, 0)

    k2_count = CH // RADIX

    def pair(q, _):
        def dot(a, b):
            return lax.dot_general(a, b, CONTRACT_LANES, preferred_element_type=jnp.float32)

        high, low = high_ref[q], low_ref[q]
        out = dot(high, y_high[q]) + dot(high, y_low[q]) + dot(low, y_high[q])
        mirror = jnp.where(q == 0, PAIRS, RADIX - q)
        for side, residue in enumerate((q, mirror)):
            for ri in range(2):
                for i in range(inputs):
                    first = (side * 2 + ri) * k2_count
                    block = out[first : first + k2_count, i * spec : (i + 1) * spec]
                    start = residue * 8 + ri * inputs + i
                    wide[pl.ds(start, k2_count, stride=RADIX * 8), :] = block
        return 0

    lax.fori_loop(0, PAIRS, pair, 0)

    pl.semaphore_wait(all_in, line - 1)

    def pack_and_send(step, _):
        peer = lax.rem(chan + step, chans)
        rows_at = pl.ds(pl.multiple_of(peer * (RADIX * 8), RADIX * 8), RADIX * 8)
        packed = wide[rows_at, :].astype(jnp.bfloat16)
        sent[pl.ds(peer * times, times)] = packed.reshape(times, RADIX // times, 8, LANES)
        for step_t in range(times):
            peer_t = lax.rem(tm + step_t, times)
            source = sent.at[peer * times + peer_t]
            target = got_ref.at[:, tm, chan]

            def remote():
                pltpu.make_async_remote_copy(
                    source, target, send_sem, recv_sem,
                    device_id=(peer, peer_t), device_id_type=MESH,
                ).start()

            if step_t == 0:

                @pl.when(step == 0)
                def _():
                    pltpu.make_async_copy(source, target, own_sem).start()

                pl.when(step > 0)(remote)
            else:
                remote()
        return 0

    lax.fori_loop(0, chans, pack_and_send, 0)

    pltpu.make_async_copy(sent.at[0], sent.at[0], own_sem).wait()
    others = sent.at[pl.ds(0, total - 1)]
    pltpu.make_async_copy(others, others, send_sem).wait()
    pltpu.make_async_copy(others, others, recv_sem).wait()

    @pl.when(tm < times - 1)
    def _():
        pltpu.make_async_copy(tail_out, tail_out, halo_send).wait()


def gram_kernel(scale, got_ref, vis_ref):
    times = got_ref.shape[1]
    lower = lax.broadcasted_iota(jnp.int32, (1, 8, LANES), 1) < 4
    real, imag = [], []
    for t in range(times):
        block = got_ref[0, t].astype(jnp.float32)
        pairs = block.reshape(block.shape[0] // 2, 2, 8, LANES)
        a, b = pairs[:, 0], pairs[:, 1]
        re = jnp.where(lower, a, pltpu.roll(b, 4, 1))
        im = jnp.where(lower, pltpu.roll(a, 4, 1), b)
        real.append(re.reshape(-1, LANES).astype(jnp.bfloat16))
        imag.append(im.reshape(-1, LANES).astype(jnp.bfloat16))
    both = jnp.concatenate(real + imag, axis=1)
    turned = jnp.concatenate(imag + [-part for part in real], axis=1)
    for part, left in enumerate((both, turned)):
        gram = lax.dot_general(left, both, CONTRACT_LANES, preferred_element_type=jnp.float32)
        vis_ref[0, part] = gram * scale


def body(samples):
    chans = lax.axis_size("chan")
    times = lax.axis_size("tm")
    inputs = samples.shape[0]
    spec = samples.shape[1] // (2 * CH)
    rows = RADIX * inputs
    own_chans = CH // (chans * times)
    arranged = samples.reshape(inputs, spec, RADIX, LANES).transpose(1, 2, 0, 3)
    arranged = arranged.reshape(spec, rows, LANES)
    high, low = fourier_tables()
    vmem = pl.BlockSpec(memory_space=pltpu.VMEM)
    got_shape = (own_chans, times, chans, 2 * inputs, LANES)
    got = pl.pallas_call(
        functools.partial(spectra_kernel, chans, times, inputs, spec),
        out_shape=jax.ShapeDtypeStruct(got_shape, jnp.bfloat16),
        in_specs=[pl.BlockSpec(memory_space=pl.ANY), vmem, vmem, vmem],
        out_specs=vmem,
        scratch_shapes=[
            pltpu.VMEM((spec, rows, LANES), jnp.int32),
            pltpu.VMEM((TAPS - 1, rows, LANES), jnp.int32),
            pltpu.VMEM((TAPS - 1, rows, LANES), jnp.bfloat16),
            pltpu.VMEM((TAPS - 1, rows, LANES), jnp.bfloat16),
            pltpu.VMEM((TAPS - 1, rows, LANES), jnp.float32),
            pltpu.VMEM((rows * spec, LANES), jnp.float32),
            pltpu.VMEM((PAIRS, inputs * spec, 2 * LANES), jnp.bfloat16),
            pltpu.VMEM((PAIRS, inputs * spec, 2 * LANES), jnp.bfloat16),
            pltpu.VMEM((chans * times, own_chans, 2 * inputs, LANES), jnp.bfloat16),
            pltpu.SemaphoreType.DMA((rows // 8,)),
        ]
        + [pltpu.SemaphoreType.DMA] * 6
        + [pltpu.SemaphoreType.REGULAR],
        compiler_params=pltpu.CompilerParams(
            collective_id=0, has_side_effects=True, vmem_limit_bytes=48 << 20
        ),
    )(arranged, jnp.asarray(filter_table(inputs)), jnp.asarray(high), jnp.asarray(low))
    scale = float(np.float32(1.0 / (NOISE_POWER * spec * times)))
    return pl.pallas_call(
        functools.partial(gram_kernel, scale),
        grid=(own_chans,),
        out_shape=jax.ShapeDtypeStruct((own_chans, 2, chans * inputs, chans * inputs), jnp.float32),
        in_specs=[pl.BlockSpec((1, *got_shape[1:]), lambda j: (j, 0, 0, 0, 0))],
        out_specs=pl.BlockSpec(
            (1, 2, chans * inputs, chans * inputs), lambda j: (j, 0, 0, 0)
        ),
    )(got)


def solution(mesh):
    return jax.shard_map(
        body,
        mesh=mesh,
        in_specs=(P("chan", "tm"),),
        out_specs=P(("chan", "tm"), None, None, None),
        check_vma=False,
    )
```

```python
import functools

import jax
import jax.numpy as jnp
import numpy as np
from jax import lax
from jax.experimental import pallas as pl
from jax.experimental.pallas import tpu as pltpu
from jax.sharding import PartitionSpec as P

CH = 1024
TAPS = 16
NOISE_POWER = 21.25
MESH = pl.DeviceIdType.MESH
LANES = 128
RADIX = 2 * CH // LANES
PAIRS = RADIX // 2
CONTRACT_LANES = (((1,), (1,)), ((), ()))


def filter_table(inputs):
    frame_len = 2 * CH
    position = (TAPS - 1 - np.arange(TAPS))[:, None] * frame_len + np.arange(frame_len)[None, :]
    argument = (position - TAPS * frame_len / 2) / frame_len
    window = 0.5 - 0.5 * np.cos(2.0 * np.pi * position / (TAPS * frame_len))
    weights = (np.sinc(argument) * window).astype(np.float32)
    weights = weights.reshape(TAPS, RADIX, 1, LANES)
    return np.broadcast_to(weights, (TAPS, RADIX, inputs, LANES)).reshape(TAPS, -1, LANES)


def fourier_tables():
    table = np.zeros((PAIRS, 2, 2, CH // RADIX, 2, LANES), np.float64)
    lane = np.arange(LANES)[None, :]
    for q in range(PAIRS):
        for side in range(2):
            residue = (q, RADIX - q if q else PAIRS)[side]
            chan = residue + RADIX * np.arange(CH // RADIX)[:, None]
            angle = 2.0 * np.pi * (chan * lane % (2 * CH)) / (2 * CH)
            cos, sin = np.cos(angle), np.sin(angle)
            if q == 0:
                table[q, side, 0, :, side] = cos
                table[q, side, 1, :, side] = -sin
            else:
                sign = (1, -1)[side]
                table[q, side, 0, :, 0] = cos
                table[q, side, 0, :, 1] = sign * sin
                table[q, side, 1, :, 0] = -sin
                table[q, side, 1, :, 1] = sign * cos
    table = (table / np.sqrt(2.0 * CH)).reshape(PAIRS, 2 * LANES, 2 * LANES).astype(np.float32)
    high = table.astype(jnp.bfloat16)
    low = (table - high.astype(np.float32)).astype(jnp.bfloat16)
    return high, low


def first_stage(x):
    a = [x[n] + x[n + 8] for n in range(8)]
    b = [x[n] - x[n + 8] for n in range(8)]
    out = [None] * 8
    aa = [a[n] + a[n + 4] for n in range(4)]
    ab = [a[n] - a[n + 4] for n in range(4)]
    even, odd = aa[0] + aa[2], aa[1] + aa[3]
    out[0] = (even + odd, even - odd)
    out[4] = (aa[0] - aa[2], aa[3] - aa[1])
    root = float(np.sqrt(0.5))
    plus, minus = (ab[1] + ab[3]) * root, (ab[1] - ab[3]) * root
    out[2] = (ab[0] + minus, -(ab[2] + plus))
    out[6] = (ab[0] - minus, ab[2] - plus)
    d = [b[n] - b[8 - n] for n in range(1, 4)]
    e = [b[n] + b[8 - n] for n in range(1, 4)]
    for k in (1, 3, 5, 7):
        re = b[0]
        im = -b[4] if k % 4 == 1 else b[4]
        for n in range(1, 4):
            re = re + d[n - 1] * float(np.cos(np.pi * k * n / 8))
            im = im - e[n - 1] * float(np.sin(np.pi * k * n / 8))
        out[k] = (re, im)
    return out


ORDER = ((1, ()), (0, (0,)), (7, (8,)), (5, ()), (4, (4,)), (3, (12,)), (2, (2, 14)), (6, (6, 10)))
EARLY_GROUPS = 3


def channel_gram(blocks, index, scale):
    lower = lax.broadcasted_iota(jnp.int32, (1, 8, LANES), 1) < 4
    real, imag = [], []
    for block in blocks:
        rows = block[:, index * 8 : index * 8 + 8].astype(jnp.float32)
        pairs = rows.reshape(rows.shape[0] // 2, 2, 8, LANES)
        a, b = pairs[:, 0], pairs[:, 1]
        re = jnp.where(lower, a, pltpu.roll(b, 4, 1))
        im = jnp.where(lower, pltpu.roll(a, 4, 1), b)
        real.append(re.reshape(-1, LANES).astype(jnp.bfloat16))
        imag.append(im.reshape(-1, LANES).astype(jnp.bfloat16))
    both = jnp.concatenate(real + imag, axis=1)
    turned = jnp.concatenate(imag + [-part for part in real], axis=1)
    return [
        lax.dot_general(left, both, CONTRACT_LANES, preferred_element_type=jnp.float32) * scale
        for left in (both, turned)
    ]


def spectra_kernel(
    chans, times, inputs, spec, scale,
    x_hbm, w_hbm, high_hbm, low_hbm, early_ref, late_ref,
    x_buf, w_ref, high_ref, low_ref, tail_buf, tail_out, halo, halo_wide, wide, y_high, y_low,
    sent, first_got,
    x_sem, table_sem, tail_sem, halo_send, halo_recv, send_sem, recv_sem, own_sem, all_in,
):
    total = chans * times
    ahead = TAPS - 1
    rows = RADIX * inputs
    groups = rows // 8
    chan, tm = lax.axis_index("chan"), lax.axis_index("tm")
    barrier = pltpu.get_barrier_semaphore()

    line = chans // times
    row, column = chan // times, chan % times * times + tm

    def row_peer(step):
        at = lax.rem(column + step, line)
        return (row * times + at // times, at % times)

    def column_peer(step):
        return (lax.rem(row + step, line) * times + chan % times, tm)

    def signal(semaphore, peer):
        pl.semaphore_signal(semaphore, inc=1, device_id=peer, device_id_type=MESH)

    def piece(g):
        part = pl.ds(pl.multiple_of(g * 8, 8), 8)
        return pltpu.make_async_copy(x_hbm.at[:, part], x_buf.at[:, part], x_sem.at[g])

    weights_copy = pltpu.make_async_copy(w_hbm, w_ref, table_sem.at[0])
    high_copy = pltpu.make_async_copy(high_hbm, high_ref, table_sem.at[1])
    low_copy = pltpu.make_async_copy(low_hbm, low_ref, table_sem.at[2])
    tail_copy = pltpu.make_async_copy(x_hbm.at[pl.ds(spec - ahead, ahead)], tail_buf, tail_sem)
    weights_copy.start()
    piece(0).start()
    tail_copy.start()
    for g in range(1, groups):
        piece(g).start()
    high_copy.start()
    low_copy.start()

    for step in range(1, line):
        signal(barrier, row_peer(step))
        signal(barrier, column_peer(step))

    def filtered(taps, window, base, fresh, r0):
        seq = list(window) + fresh
        for j in range(TAPS):
            acc = taps[0] * seq[ahead + j]
            for p in range(1, TAPS):
                acc = acc + taps[p] * seq[ahead + j - p]
            wide[pl.ds(r0 * spec + base + j, 8, stride=spec), :] = acc
        return tuple(seq[TAPS:])

    def frame(s, r0):
        return x_buf[s, pl.ds(r0, 8), :].astype(jnp.float32)

    def tap_rows(r0):
        return [w_ref[p, pl.ds(r0, 8), :] for p in range(TAPS)]

    def own_frames(g, _):
        r0 = pl.multiple_of(g * 8, 8)
        piece(g).wait()
        taps = tap_rows(r0)
        window = tuple(frame(s, r0) for s in range(1, TAPS))

        def block(n, window):
            base = TAPS + n * TAPS
            fresh = [frame(base + j, r0) for j in range(TAPS)]
            return filtered(taps, window, base, fresh, r0)

        lax.fori_loop(0, spec // TAPS - 1, block, window)
        return 0

    weights_copy.wait()
    tail_copy.wait()
    for f in range(ahead):
        tail_out[f] = tail_buf[f].astype(jnp.float32).astype(jnp.bfloat16)
    lax.fori_loop(0, EARLY_GROUPS, own_frames, 0)

    pl.semaphore_wait(barrier, 2 * (line - 1))

    @pl.when(tm < times - 1)
    def _():
        pltpu.make_async_remote_copy(
            tail_out, halo, halo_send, halo_recv,
            device_id=(chan, lax.rem(tm + 1, times)), device_id_type=MESH,
        ).start()

    for step in range(1, line):
        signal(all_in, column_peer(step))

    lax.fori_loop(EARLY_GROUPS, groups, own_frames, 0)

    @pl.when(tm > 0)
    def _():
        pltpu.make_async_copy(halo, halo, halo_recv).wait()
        for f in range(ahead):
            halo_wide[f] = halo[f].astype(jnp.float32)

    @pl.when(tm == 0)
    def _():
        for f in range(ahead):
            halo_wide[f] = jnp.zeros((rows, LANES), jnp.float32)

    def first_frames(g, _):
        r0 = pl.multiple_of(g * 8, 8)
        window = [halo_wide[f, pl.ds(r0, 8), :] for f in range(ahead)]
        filtered(tap_rows(r0), window, 0, [frame(j, r0) for j in range(TAPS)], r0)
        return 0

    lax.fori_loop(0, groups, first_frames, 0)

    def butterflies(n, _):
        i, s0 = n // (spec // 16), n % (spec // 16) * 16
        x = [
            wide[pl.ds(pl.multiple_of((row * inputs + i) * spec + s0, 16), 16), :]
            for row in range(RADIX)
        ]
        place = pl.ds(pl.multiple_of(i * spec + s0, 16), 16)
        for q, parts in enumerate(first_stage(x)):
            for part, value in enumerate(parts):
                lanes = pl.ds(part * LANES, LANES)
                high = value.astype(jnp.bfloat16)
                y_high[q, place, lanes] = high
                y_low[q, place, lanes] = (value - high.astype(jnp.float32)).astype(jnp.bfloat16)
        return 0

    lax.fori_loop(0, inputs * spec // 16, butterflies, 0)

    high_copy.wait()
    low_copy.wait()
    pl.semaphore_wait(all_in, line - 1)

    k2_count = CH // RADIX

    def transform(q):
        def dot(a, b):
            return lax.dot_general(a, b, CONTRACT_LANES, preferred_element_type=jnp.float32)

        high, low = high_ref[q], low_ref[q]
        out = dot(high, y_high[q]) + dot(high, y_low[q]) + dot(low, y_high[q])
        for side, residue in enumerate((q, RADIX - q if q else PAIRS)):
            for ri in range(2):
                for i in range(inputs):
                    first = (side * 2 + ri) * k2_count
                    block = out[first : first + k2_count, i * spec : (i + 1) * spec]
                    start = residue * 8 + ri * inputs + i
                    wide[pl.ds(start, k2_count, stride=RADIX * 8), :] = block

    def pack(peer, residue):
        at = pl.ds(pl.multiple_of(peer * (RADIX * 8) + residue * 8, 16), 16)
        place = peer * PAIRS + residue // 2
        sent[place] = wide[at, :].astype(jnp.bfloat16)
        return sent.at[place]

    def deliver(residue):
        peer_t, half = residue // times, residue // 2 % 2
        target = (first_got, late_ref)[half].at[tm, chan]

        def remote(peer, source):
            pltpu.make_async_remote_copy(
                source, target, send_sem, recv_sem.at[half],
                device_id=(peer, peer_t), device_id_type=MESH,
            ).start()

        own = pack(chan, residue)

        @pl.when(tm == peer_t)
        def _():
            pltpu.make_async_copy(own, target, own_sem.at[half]).start()

        @pl.when(tm != peer_t)
        def _():
            remote(chan, own)

        def one(step, _):
            peer = lax.rem(chan + step, chans)
            remote(peer, pack(peer, residue))
            return 0

        lax.fori_loop(1, chans, one, 0)

    for q, complete in ORDER:
        transform(q)
        for residue in complete:
            deliver(residue)

    others = sent.at[pl.ds(0, total - 1)]

    def arrived(half):
        pltpu.make_async_copy(sent.at[0], sent.at[0], own_sem.at[half]).wait()
        pltpu.make_async_copy(others, others, recv_sem.at[half]).wait()

    arrived(0)
    for index in range(2):
        parts = channel_gram([first_got[t] for t in range(times)], index, scale)
        for part, value in enumerate(parts):
            early_ref[index, part] = value
    arrived(1)
    both_halves = sent.at[pl.ds(0, 2 * (total - 1))]
    pltpu.make_async_copy(both_halves, both_halves, send_sem).wait()

    @pl.when(tm < times - 1)
    def _():
        pltpu.make_async_copy(tail_out, tail_out, halo_send).wait()


def late_kernel(scale, early_ref, got_ref, vis_ref, late, early_sem, late_sem):
    early_copy = pltpu.make_async_copy(early_ref, vis_ref.at[pl.ds(0, 2)], early_sem)
    early_copy.start()
    copies = []
    for index in range(2):
        parts = channel_gram([got_ref[t] for t in range(got_ref.shape[0])], index, scale)
        for part, value in enumerate(parts):
            late[index, part] = value
        copies.append(
            pltpu.make_async_copy(late.at[index], vis_ref.at[2 + index], late_sem.at[index])
        )
        copies[-1].start()
    early_copy.wait()
    for copy in copies:
        copy.wait()


def body(samples):
    chans = lax.axis_size("chan")
    times = lax.axis_size("tm")
    inputs = samples.shape[0]
    spec = samples.shape[1] // (2 * CH)
    rows = RADIX * inputs
    all_inputs = chans * inputs
    arranged = samples.reshape(inputs, spec, RADIX, LANES).transpose(1, 2, 0, 3)
    arranged = arranged.reshape(spec, rows, LANES)
    weights = jnp.asarray(filter_table(inputs))
    high, low = (jnp.asarray(table) for table in fourier_tables())
    vmem = pl.BlockSpec(memory_space=pltpu.VMEM)
    hbm = pl.BlockSpec(memory_space=pltpu.HBM)
    scale = float(np.float32(1.0 / (NOISE_POWER * spec * times)))
    got_shape = (times, chans, 4 * inputs, LANES)
    vis_shape = (2, 2, all_inputs, all_inputs)
    early, got = pl.pallas_call(
        functools.partial(spectra_kernel, chans, times, inputs, spec, scale),
        out_shape=(
            jax.ShapeDtypeStruct(vis_shape, jnp.float32),
            jax.ShapeDtypeStruct(got_shape, jnp.bfloat16),
        ),
        in_specs=[hbm] * 4,
        out_specs=(vmem, vmem),
        scratch_shapes=[
            pltpu.VMEM((spec, rows, LANES), jnp.int32),
            pltpu.VMEM(weights.shape, jnp.float32),
            pltpu.VMEM(high.shape, jnp.bfloat16),
            pltpu.VMEM(low.shape, jnp.bfloat16),
            pltpu.VMEM((TAPS - 1, rows, LANES), jnp.int32),
            pltpu.VMEM((TAPS - 1, rows, LANES), jnp.bfloat16),
            pltpu.VMEM((TAPS - 1, rows, LANES), jnp.bfloat16),
            pltpu.VMEM((TAPS - 1, rows, LANES), jnp.float32),
            pltpu.VMEM((rows * spec, LANES), jnp.float32),
            pltpu.VMEM((PAIRS, inputs * spec, 2 * LANES), jnp.bfloat16),
            pltpu.VMEM((PAIRS, inputs * spec, 2 * LANES), jnp.bfloat16),
            pltpu.VMEM((chans * PAIRS, 4 * inputs, LANES), jnp.bfloat16),
            pltpu.VMEM(got_shape, jnp.bfloat16),
            pltpu.SemaphoreType.DMA((rows // 8,)),
            pltpu.SemaphoreType.DMA((3,)),
            pltpu.SemaphoreType.DMA,
            pltpu.SemaphoreType.DMA,
            pltpu.SemaphoreType.DMA,
            pltpu.SemaphoreType.DMA,
            pltpu.SemaphoreType.DMA((2,)),
            pltpu.SemaphoreType.DMA((2,)),
            pltpu.SemaphoreType.REGULAR,
        ],
        compiler_params=pltpu.CompilerParams(
            collective_id=0, has_side_effects=True, vmem_limit_bytes=48 << 20
        ),
    )(arranged, *(pltpu.with_memory_space_constraint(v, pltpu.HBM) for v in (weights, high, low)))
    return pl.pallas_call(
        functools.partial(late_kernel, scale),
        out_shape=jax.ShapeDtypeStruct((4, *vis_shape[1:]), jnp.float32),
        in_specs=[vmem, vmem],
        out_specs=hbm,
        scratch_shapes=[
            pltpu.VMEM(vis_shape, jnp.float32),
            pltpu.SemaphoreType.DMA,
            pltpu.SemaphoreType.DMA((2,)),
        ],
        compiler_params=pltpu.CompilerParams(vmem_limit_bytes=40 << 20),
    )(early, got)


def solution(mesh):
    return jax.shard_map(
        body,
        mesh=mesh,
        in_specs=(P("chan", "tm"),),
        out_specs=P(("chan", "tm"), None, None, None),
        check_vma=False,
    )
```

```python
import functools

import jax
import jax.numpy as jnp
import numpy as np
from jax import lax
from jax.experimental import pallas as pl
from jax.experimental.pallas import tpu as pltpu
from jax.sharding import PartitionSpec as P

CH = 1024
TAPS = 16
NOISE_POWER = 21.25
MESH = pl.DeviceIdType.MESH
LANES = 128
RADIX = 2 * CH // LANES
PAIRS = RADIX // 2
CONTRACT_LANES = (((1,), (1,)), ((), ()))


def filter_table(inputs):
    frame_len = 2 * CH
    position = (TAPS - 1 - np.arange(TAPS))[:, None] * frame_len + np.arange(frame_len)[None, :]
    argument = (position - TAPS * frame_len / 2) / frame_len
    window = 0.5 - 0.5 * np.cos(2.0 * np.pi * position / (TAPS * frame_len))
    weights = (np.sinc(argument) * window).astype(np.float32)
    weights = weights.reshape(TAPS, RADIX, 1, LANES)
    return np.broadcast_to(weights, (TAPS, RADIX, inputs, LANES)).reshape(TAPS, -1, LANES)


def fourier_tables():
    table = np.zeros((PAIRS, 2, 2, CH // RADIX, 2, LANES), np.float64)
    lane = np.arange(LANES)[None, :]
    for q in range(PAIRS):
        for side in range(2):
            residue = (q, RADIX - q if q else PAIRS)[side]
            chan = residue + RADIX * np.arange(CH // RADIX)[:, None]
            angle = 2.0 * np.pi * (chan * lane % (2 * CH)) / (2 * CH)
            cos, sin = np.cos(angle), np.sin(angle)
            if q == 0:
                table[q, side, 0, :, side] = cos
                table[q, side, 1, :, side] = -sin
            else:
                sign = (1, -1)[side]
                table[q, side, 0, :, 0] = cos
                table[q, side, 0, :, 1] = sign * sin
                table[q, side, 1, :, 0] = -sin
                table[q, side, 1, :, 1] = sign * cos
    table = (table / np.sqrt(2.0 * CH)).reshape(PAIRS, 2 * LANES, 2 * LANES).astype(np.float32)
    high = table.astype(jnp.bfloat16)
    low = (table - high.astype(np.float32)).astype(jnp.bfloat16)
    return high, low


def first_stage(x):
    a = [x[n] + x[n + 8] for n in range(8)]
    b = [x[n] - x[n + 8] for n in range(8)]
    out = [None] * 8
    aa = [a[n] + a[n + 4] for n in range(4)]
    ab = [a[n] - a[n + 4] for n in range(4)]
    even, odd = aa[0] + aa[2], aa[1] + aa[3]
    out[0] = (even + odd, even - odd)
    out[4] = (aa[0] - aa[2], aa[3] - aa[1])
    root = float(np.sqrt(0.5))
    plus, minus = (ab[1] + ab[3]) * root, (ab[1] - ab[3]) * root
    out[2] = (ab[0] + minus, -(ab[2] + plus))
    out[6] = (ab[0] - minus, ab[2] - plus)
    d = [b[n] - b[8 - n] for n in range(1, 4)]
    e = [b[n] + b[8 - n] for n in range(1, 4)]
    for k in (1, 3, 5, 7):
        re = b[0]
        im = -b[4] if k % 4 == 1 else b[4]
        for n in range(1, 4):
            re = re + d[n - 1] * float(np.cos(np.pi * k * n / 8))
            im = im - e[n - 1] * float(np.sin(np.pi * k * n / 8))
        out[k] = (re, im)
    return out


ORDER = ((1, ()), (0, (0,)), (7, (8,)), (5, ()), (4, (4,)), (3, (12,)), (2, (2, 14)), (6, (6, 10)))
EARLY_GROUPS = 5


def channel_gram(blocks, index, scale):
    lower = lax.broadcasted_iota(jnp.int32, (1, 8, LANES), 1) < 4
    real, imag = [], []
    for block in blocks:
        rows = block[:, index * 8 : index * 8 + 8].astype(jnp.float32)
        pairs = rows.reshape(rows.shape[0] // 2, 2, 8, LANES)
        a, b = pairs[:, 0], pairs[:, 1]
        re = jnp.where(lower, a, pltpu.roll(b, 4, 1))
        im = jnp.where(lower, pltpu.roll(a, 4, 1), b)
        real.append(re.reshape(-1, LANES).astype(jnp.bfloat16))
        imag.append(im.reshape(-1, LANES).astype(jnp.bfloat16))
    both = jnp.concatenate(real + imag, axis=1)
    turned = jnp.concatenate(imag + [-part for part in real], axis=1)
    return [
        lax.dot_general(left, both, CONTRACT_LANES, preferred_element_type=jnp.float32) * scale
        for left in (both, turned)
    ]


def spectra_kernel(
    chans, times, inputs, spec, scale,
    x_hbm, w_hbm, high_hbm, low_hbm, early_ref, late_ref,
    x_buf, w_ref, high_ref, low_ref, tail_buf, tail_out, halo, halo_wide, wide, y_high, y_low,
    sent, first_got,
    x_sem, table_sem, tail_sem, halo_send, halo_recv, send_sem, recv_sem, own_sem, all_in,
):
    total = chans * times
    ahead = TAPS - 1
    rows = RADIX * inputs
    groups = rows // 8
    chan, tm = lax.axis_index("chan"), lax.axis_index("tm")
    barrier = pltpu.get_barrier_semaphore()

    line = chans // times
    row, column = chan // times, chan % times * times + tm

    def row_peer(step):
        at = lax.rem(column + step, line)
        return (row * times + at // times, at % times)

    def column_peer(step):
        return (lax.rem(row + step, line) * times + chan % times, tm)

    def signal(semaphore, peer):
        pl.semaphore_signal(semaphore, inc=1, device_id=peer, device_id_type=MESH)

    def piece(g):
        part = pl.ds(pl.multiple_of(g * 8, 8), 8)
        return pltpu.make_async_copy(x_hbm.at[:, part], x_buf.at[:, part], x_sem.at[g])

    weights_copy = pltpu.make_async_copy(w_hbm, w_ref, table_sem.at[0])
    high_copy = pltpu.make_async_copy(high_hbm, high_ref, table_sem.at[1])
    low_copy = pltpu.make_async_copy(low_hbm, low_ref, table_sem.at[2])
    tail_copy = pltpu.make_async_copy(x_hbm.at[pl.ds(spec - ahead, ahead)], tail_buf, tail_sem)
    weights_copy.start()
    piece(0).start()
    tail_copy.start()
    for g in range(1, groups):
        piece(g).start()
    high_copy.start()
    low_copy.start()

    for step in range(1, line):
        signal(barrier, row_peer(step))
    for step in range(1, line):
        signal(barrier, column_peer(step))

    def filtered(taps, window, base, fresh, r0):
        seq = list(window) + fresh
        for j in range(TAPS):
            acc = taps[0] * seq[ahead + j]
            for p in range(1, TAPS):
                acc = acc + taps[p] * seq[ahead + j - p]
            wide[pl.ds(r0 * spec + base + j, 8, stride=spec), :] = acc
        return tuple(seq[TAPS:])

    def frame(s, r0):
        return x_buf[s, pl.ds(r0, 8), :].astype(jnp.float32)

    def tap_rows(r0):
        return [w_ref[p, pl.ds(r0, 8), :] for p in range(TAPS)]

    def own_frames(g, _):
        r0 = pl.multiple_of(g * 8, 8)
        piece(g).wait()
        taps = tap_rows(r0)
        window = tuple(frame(s, r0) for s in range(1, TAPS))

        def block(n, window):
            base = TAPS + n * TAPS
            fresh = [frame(base + j, r0) for j in range(TAPS)]
            return filtered(taps, window, base, fresh, r0)

        lax.fori_loop(0, spec // TAPS - 1, block, window)
        return 0

    weights_copy.wait()
    lax.fori_loop(0, EARLY_GROUPS, own_frames, 0)
    tail_copy.wait()
    for f in range(ahead):
        tail_out[f] = tail_buf[f].astype(jnp.float32).astype(jnp.bfloat16)

    pl.semaphore_wait(barrier, 2 * (line - 1))
    for step in range(1, line):
        signal(all_in, column_peer(step))

    @pl.when(tm < times - 1)
    def _():
        pltpu.make_async_remote_copy(
            tail_out, halo, halo_send, halo_recv,
            device_id=(chan, lax.rem(tm + 1, times)), device_id_type=MESH,
        ).start()

    lax.fori_loop(EARLY_GROUPS, groups, own_frames, 0)

    def butterflies(i, s0):
        x = [
            wide[pl.ds(pl.multiple_of((row * inputs + i) * spec + s0, 16), 16), :]
            for row in range(RADIX)
        ]
        place = pl.ds(pl.multiple_of(i * spec + s0, 16), 16)
        for q, parts in enumerate(first_stage(x)):
            for part, value in enumerate(parts):
                lanes = pl.ds(part * LANES, LANES)
                high = value.astype(jnp.bfloat16)
                y_high[q, place, lanes] = high
                y_low[q, place, lanes] = (value - high.astype(jnp.float32)).astype(jnp.bfloat16)
        return 0

    later = spec // 16 - 1
    lax.fori_loop(
        0, inputs * later, lambda n, _: butterflies(n // later, (n % later + 1) * 16), 0
    )

    @pl.when(tm > 0)
    def _():
        pltpu.make_async_copy(halo, halo, halo_recv).wait()
        for f in range(ahead):
            halo_wide[f] = halo[f].astype(jnp.float32)

    @pl.when(tm == 0)
    def _():
        for f in range(ahead):
            halo_wide[f] = jnp.zeros((rows, LANES), jnp.float32)

    def first_frames(g, _):
        r0 = pl.multiple_of(g * 8, 8)
        window = [halo_wide[f, pl.ds(r0, 8), :] for f in range(ahead)]
        filtered(tap_rows(r0), window, 0, [frame(j, r0) for j in range(TAPS)], r0)
        return 0

    lax.fori_loop(0, groups, first_frames, 0)
    lax.fori_loop(0, inputs, lambda i, _: butterflies(i, 0), 0)

    high_copy.wait()
    low_copy.wait()
    pl.semaphore_wait(all_in, line - 1)

    k2_count = CH // RADIX

    def transform(q):
        def dot(a, b):
            return lax.dot_general(a, b, CONTRACT_LANES, preferred_element_type=jnp.float32)

        high, low = high_ref[q], low_ref[q]
        out = dot(high, y_high[q]) + dot(high, y_low[q]) + dot(low, y_high[q])
        for side, residue in enumerate((q, RADIX - q if q else PAIRS)):
            for ri in range(2):
                for i in range(inputs):
                    first = (side * 2 + ri) * k2_count
                    block = out[first : first + k2_count, i * spec : (i + 1) * spec]
                    start = residue * 8 + ri * inputs + i
                    wide[pl.ds(start, k2_count, stride=RADIX * 8), :] = block

    def pack(peer, residue):
        at = pl.ds(pl.multiple_of(peer * (RADIX * 8) + residue * 8, 16), 16)
        place = peer * PAIRS + residue // 2
        sent[place] = wide[at, :].astype(jnp.bfloat16)
        return sent.at[place]

    def deliver(residue):
        peer_t, half = residue // times, residue // 2 % 2
        target = (first_got, late_ref)[half].at[tm, chan]

        def remote(peer, source):
            pltpu.make_async_remote_copy(
                source, target, send_sem, recv_sem.at[half],
                device_id=(peer, peer_t), device_id_type=MESH,
            ).start()

        own = pack(chan, residue)

        @pl.when(tm == peer_t)
        def _():
            pltpu.make_async_copy(own, target, own_sem.at[half]).start()

        @pl.when(tm != peer_t)
        def _():
            remote(chan, own)

        def one(step, _):
            peer = lax.rem(chan + step, chans)
            remote(peer, pack(peer, residue))
            return 0

        lax.fori_loop(1, chans, one, 0)

    for q, complete in ORDER:
        transform(q)
        for residue in complete:
            deliver(residue)

    others = sent.at[pl.ds(0, total - 1)]

    def arrived(half):
        pltpu.make_async_copy(sent.at[0], sent.at[0], own_sem.at[half]).wait()
        pltpu.make_async_copy(others, others, recv_sem.at[half]).wait()

    arrived(0)
    for index in range(2):
        parts = channel_gram([first_got[t] for t in range(times)], index, scale)
        for part, value in enumerate(parts):
            early_ref[index, part] = value
    arrived(1)
    both_halves = sent.at[pl.ds(0, 2 * (total - 1))]
    pltpu.make_async_copy(both_halves, both_halves, send_sem).wait()

    @pl.when(tm < times - 1)
    def _():
        pltpu.make_async_copy(tail_out, tail_out, halo_send).wait()


def late_kernel(scale, early_ref, got_ref, vis_ref, late, early_sem, late_sem):
    early_copy = pltpu.make_async_copy(early_ref, vis_ref.at[pl.ds(0, 2)], early_sem)
    early_copy.start()
    copies = []
    for index in range(2):
        parts = channel_gram([got_ref[t] for t in range(got_ref.shape[0])], index, scale)
        for part, value in enumerate(parts):
            late[index, part] = value
        copies.append(
            pltpu.make_async_copy(late.at[index], vis_ref.at[2 + index], late_sem.at[index])
        )
        copies[-1].start()
    early_copy.wait()
    for copy in copies:
        copy.wait()


def body(samples):
    chans = lax.axis_size("chan")
    times = lax.axis_size("tm")
    inputs = samples.shape[0]
    spec = samples.shape[1] // (2 * CH)
    rows = RADIX * inputs
    all_inputs = chans * inputs
    arranged = samples.reshape(inputs, spec, RADIX, LANES).transpose(1, 2, 0, 3)
    arranged = arranged.reshape(spec, rows, LANES)
    weights = jnp.asarray(filter_table(inputs))
    high, low = (jnp.asarray(table) for table in fourier_tables())
    vmem = pl.BlockSpec(memory_space=pltpu.VMEM)
    hbm = pl.BlockSpec(memory_space=pltpu.HBM)
    scale = float(np.float32(1.0 / (NOISE_POWER * spec * times)))
    got_shape = (times, chans, 4 * inputs, LANES)
    vis_shape = (2, 2, all_inputs, all_inputs)
    early, got = pl.pallas_call(
        functools.partial(spectra_kernel, chans, times, inputs, spec, scale),
        out_shape=(
            jax.ShapeDtypeStruct(vis_shape, jnp.float32),
            jax.ShapeDtypeStruct(got_shape, jnp.bfloat16),
        ),
        in_specs=[hbm] * 4,
        out_specs=(vmem, vmem),
        scratch_shapes=[
            pltpu.VMEM((spec, rows, LANES), jnp.int32),
            pltpu.VMEM(weights.shape, jnp.float32),
            pltpu.VMEM(high.shape, jnp.bfloat16),
            pltpu.VMEM(low.shape, jnp.bfloat16),
            pltpu.VMEM((TAPS - 1, rows, LANES), jnp.int32),
            pltpu.VMEM((TAPS - 1, rows, LANES), jnp.bfloat16),
            pltpu.VMEM((TAPS - 1, rows, LANES), jnp.bfloat16),
            pltpu.VMEM((TAPS - 1, rows, LANES), jnp.float32),
            pltpu.VMEM((rows * spec, LANES), jnp.float32),
            pltpu.VMEM((PAIRS, inputs * spec, 2 * LANES), jnp.bfloat16),
            pltpu.VMEM((PAIRS, inputs * spec, 2 * LANES), jnp.bfloat16),
            pltpu.VMEM((chans * PAIRS, 4 * inputs, LANES), jnp.bfloat16),
            pltpu.VMEM(got_shape, jnp.bfloat16),
            pltpu.SemaphoreType.DMA((rows // 8,)),
            pltpu.SemaphoreType.DMA((3,)),
            pltpu.SemaphoreType.DMA,
            pltpu.SemaphoreType.DMA,
            pltpu.SemaphoreType.DMA,
            pltpu.SemaphoreType.DMA,
            pltpu.SemaphoreType.DMA((2,)),
            pltpu.SemaphoreType.DMA((2,)),
            pltpu.SemaphoreType.REGULAR,
        ],
        compiler_params=pltpu.CompilerParams(
            collective_id=0, has_side_effects=True, vmem_limit_bytes=48 << 20
        ),
    )(arranged, *(pltpu.with_memory_space_constraint(v, pltpu.HBM) for v in (weights, high, low)))
    return pl.pallas_call(
        functools.partial(late_kernel, scale),
        out_shape=jax.ShapeDtypeStruct((4, *vis_shape[1:]), jnp.float32),
        in_specs=[vmem, vmem],
        out_specs=hbm,
        scratch_shapes=[
            pltpu.VMEM(vis_shape, jnp.float32),
            pltpu.SemaphoreType.DMA,
            pltpu.SemaphoreType.DMA((2,)),
        ],
        compiler_params=pltpu.CompilerParams(vmem_limit_bytes=40 << 20),
    )(early, got)


def solution(mesh):
    return jax.shard_map(
        body,
        mesh=mesh,
        in_specs=(P("chan", "tm"),),
        out_specs=P(("chan", "tm"), None, None, None),
        check_vma=False,
    )
```

```python
import functools

import jax
import jax.numpy as jnp
import numpy as np
from jax import lax
from jax.experimental import pallas as pl
from jax.experimental.pallas import tpu as pltpu
from jax.sharding import PartitionSpec as P

CH = 1024
TAPS = 16
NOISE_POWER = 21.25
MESH = pl.DeviceIdType.MESH
LANES = 128
RADIX = 2 * CH // LANES
PAIRS = RADIX // 2
CONTRACT_LANES = (((1,), (1,)), ((), ()))


def filter_table(inputs):
    frame_len = 2 * CH
    position = (TAPS - 1 - np.arange(TAPS))[:, None] * frame_len + np.arange(frame_len)[None, :]
    argument = (position - TAPS * frame_len / 2) / frame_len
    window = 0.5 - 0.5 * np.cos(2.0 * np.pi * position / (TAPS * frame_len))
    weights = (np.sinc(argument) * window).astype(np.float32)
    weights = weights.reshape(TAPS, RADIX, 1, LANES)
    return np.broadcast_to(weights, (TAPS, RADIX, inputs, LANES)).reshape(TAPS, -1, LANES)


def fourier_tables():
    table = np.zeros((PAIRS, 2, 2, CH // RADIX, 2, LANES), np.float64)
    lane = np.arange(LANES)[None, :]
    for q in range(PAIRS):
        for side in range(2):
            residue = (q, RADIX - q if q else PAIRS)[side]
            chan = residue + RADIX * np.arange(CH // RADIX)[:, None]
            angle = 2.0 * np.pi * (chan * lane % (2 * CH)) / (2 * CH)
            cos, sin = np.cos(angle), np.sin(angle)
            if q == 0:
                table[q, side, 0, :, side] = cos
                table[q, side, 1, :, side] = -sin
            else:
                sign = (1, -1)[side]
                table[q, side, 0, :, 0] = cos
                table[q, side, 0, :, 1] = sign * sin
                table[q, side, 1, :, 0] = -sin
                table[q, side, 1, :, 1] = sign * cos
    table = (table / np.sqrt(2.0 * CH)).reshape(PAIRS, 2 * LANES, 2 * LANES).astype(np.float32)
    high = table.astype(jnp.bfloat16)
    low = (table - high.astype(np.float32)).astype(jnp.bfloat16)
    return high, low


def first_stage(x):
    a = [x[n] + x[n + 8] for n in range(8)]
    b = [x[n] - x[n + 8] for n in range(8)]
    out = [None] * 8
    aa = [a[n] + a[n + 4] for n in range(4)]
    ab = [a[n] - a[n + 4] for n in range(4)]
    even, odd = aa[0] + aa[2], aa[1] + aa[3]
    out[0] = (even + odd, even - odd)
    out[4] = (aa[0] - aa[2], aa[3] - aa[1])
    root = float(np.sqrt(0.5))
    plus, minus = (ab[1] + ab[3]) * root, (ab[1] - ab[3]) * root
    out[2] = (ab[0] + minus, -(ab[2] + plus))
    out[6] = (ab[0] - minus, ab[2] - plus)
    d = [b[n] - b[8 - n] for n in range(1, 4)]
    e = [b[n] + b[8 - n] for n in range(1, 4)]
    for k in (1, 3, 5, 7):
        re = b[0]
        im = -b[4] if k % 4 == 1 else b[4]
        for n in range(1, 4):
            re = re + d[n - 1] * float(np.cos(np.pi * k * n / 8))
            im = im - e[n - 1] * float(np.sin(np.pi * k * n / 8))
        out[k] = (re, im)
    return out


ORDER = ((1, ()), (0, (0,)), (7, (8,)), (5, ()), (4, (4,)), (3, (12,)), (2, (2, 14)), (6, (6, 10)))
EARLY_GROUPS = 5


def channel_gram(blocks, index, scale):
    lower = lax.broadcasted_iota(jnp.int32, (1, 8, LANES), 1) < 4
    real, imag = [], []
    for block in blocks:
        rows = block[:, index * 8 : index * 8 + 8].astype(jnp.float32)
        pairs = rows.reshape(rows.shape[0] // 2, 2, 8, LANES)
        a, b = pairs[:, 0], pairs[:, 1]
        re = jnp.where(lower, a, pltpu.roll(b, 4, 1))
        im = jnp.where(lower, pltpu.roll(a, 4, 1), b)
        real.append(re.reshape(-1, LANES).astype(jnp.bfloat16))
        imag.append(im.reshape(-1, LANES).astype(jnp.bfloat16))
    both = jnp.concatenate(real + imag, axis=1)
    turned = jnp.concatenate(imag + [-part for part in real], axis=1)
    return [
        lax.dot_general(left, both, CONTRACT_LANES, preferred_element_type=jnp.float32) * scale
        for left in (both, turned)
    ]


def spectra_kernel(
    chans, times, inputs, spec, scale,
    x_hbm, w_hbm, high_hbm, low_hbm, early_ref, late_ref,
    x_buf, w_ref, high_ref, low_ref, tail_buf, tail_out, halo, halo_wide, wide, y_high, y_low,
    sent, first_got,
    x_sem, table_sem, tail_sem, halo_send, halo_recv, send_sem, recv_sem, own_sem, all_in,
):
    total = chans * times
    ahead = TAPS - 1
    rows = RADIX * inputs
    groups = rows // 8
    chan, tm = lax.axis_index("chan"), lax.axis_index("tm")
    barrier = pltpu.get_barrier_semaphore()

    line = chans // times
    row, column = chan // times, chan % times * times + tm

    def row_peer(step):
        at = lax.rem(column + step, line)
        return (row * times + at // times, at % times)

    def column_peer(step):
        return (lax.rem(row + step, line) * times + chan % times, tm)

    def signal(semaphore, peer):
        pl.semaphore_signal(semaphore, inc=1, device_id=peer, device_id_type=MESH)

    def piece(g):
        part = pl.ds(pl.multiple_of(g * 8, 8), 8)
        return pltpu.make_async_copy(x_hbm.at[:, part], x_buf.at[:, part], x_sem.at[g])

    weights_copy = pltpu.make_async_copy(w_hbm, w_ref, table_sem.at[0])
    high_copy = pltpu.make_async_copy(high_hbm, high_ref, table_sem.at[1])
    low_copy = pltpu.make_async_copy(low_hbm, low_ref, table_sem.at[2])
    tail_copy = pltpu.make_async_copy(x_hbm.at[pl.ds(spec - ahead, ahead)], tail_buf, tail_sem)
    weights_copy.start()
    piece(0).start()
    tail_copy.start()
    for g in range(1, groups):
        piece(g).start()
    high_copy.start()
    low_copy.start()

    for step in range(1, line):
        signal(barrier, row_peer(step))
    for step in range(1, line):
        signal(barrier, column_peer(step))

    def filtered(taps, window, base, fresh, r0):
        seq = list(window) + fresh
        for j in range(TAPS):
            acc = taps[0] * seq[ahead + j]
            for p in range(1, TAPS):
                acc = acc + taps[p] * seq[ahead + j - p]
            wide[pl.ds(r0 * spec + base + j, 8, stride=spec), :] = acc
        return tuple(seq[TAPS:])

    def frame(s, r0):
        return x_buf[s, pl.ds(r0, 8), :].astype(jnp.float32)

    def tap_rows(r0):
        return [w_ref[p, pl.ds(r0, 8), :] for p in range(TAPS)]

    def own_frames(g, _):
        r0 = pl.multiple_of(g * 8, 8)
        piece(g).wait()
        taps = tap_rows(r0)
        window = tuple(frame(s, r0) for s in range(1, TAPS))

        def block(n, window):
            base = TAPS + n * TAPS
            fresh = [frame(base + j, r0) for j in range(TAPS)]
            return filtered(taps, window, base, fresh, r0)

        lax.fori_loop(0, spec // TAPS - 1, block, window)
        return 0

    weights_copy.wait()
    lax.fori_loop(0, EARLY_GROUPS, own_frames, 0)
    tail_copy.wait()
    for f in range(ahead):
        tail_out[f] = tail_buf[f].astype(jnp.float32).astype(jnp.bfloat16)

    pl.semaphore_wait(barrier, 2 * (line - 1))
    for step in range(1, line):
        signal(all_in, column_peer(step))

    @pl.when(tm < times - 1)
    def _():
        pltpu.make_async_remote_copy(
            tail_out, halo, halo_send, halo_recv,
            device_id=(chan, lax.rem(tm + 1, times)), device_id_type=MESH,
        ).start()

    lax.fori_loop(EARLY_GROUPS, groups, own_frames, 0)

    def butterflies(i, s0):
        x = [
            wide[pl.ds(pl.multiple_of((row * inputs + i) * spec + s0, 16), 16), :]
            for row in range(RADIX)
        ]
        place = pl.ds(pl.multiple_of(i * spec + s0, 16), 16)
        for q, parts in enumerate(first_stage(x)):
            for part, value in enumerate(parts):
                lanes = pl.ds(part * LANES, LANES)
                high = value.astype(jnp.bfloat16)
                y_high[q, place, lanes] = high
                y_low[q, place, lanes] = (value - high.astype(jnp.float32)).astype(jnp.bfloat16)
        return 0

    later = spec // 16 - 1
    lax.fori_loop(
        0, inputs * later, lambda n, _: butterflies(n // later, (n % later + 1) * 16), 0
    )

    @pl.when(tm > 0)
    def _():
        pltpu.make_async_copy(halo, halo, halo_recv).wait()
        for f in range(ahead):
            halo_wide[f] = halo[f].astype(jnp.float32)

    @pl.when(tm == 0)
    def _():
        for f in range(ahead):
            halo_wide[f] = jnp.zeros((rows, LANES), jnp.float32)

    def first_frames(g, _):
        r0 = pl.multiple_of(g * 8, 8)
        window = [halo_wide[f, pl.ds(r0, 8), :] for f in range(ahead)]
        filtered(tap_rows(r0), window, 0, [frame(j, r0) for j in range(TAPS)], r0)
        return 0

    lax.fori_loop(0, groups, first_frames, 0)
    lax.fori_loop(0, inputs, lambda i, _: butterflies(i, 0), 0)

    high_copy.wait()
    low_copy.wait()

    k2_count = CH // RADIX

    def transform(q):
        def dot(a, b):
            return lax.dot_general(a, b, CONTRACT_LANES, preferred_element_type=jnp.float32)

        high, low = high_ref[q], low_ref[q]
        out = dot(high, y_high[q]) + dot(high, y_low[q]) + dot(low, y_high[q])
        for side, residue in enumerate((q, RADIX - q if q else PAIRS)):
            for ri in range(2):
                for i in range(inputs):
                    first = (side * 2 + ri) * k2_count
                    block = out[first : first + k2_count, i * spec : (i + 1) * spec]
                    start = residue * 8 + ri * inputs + i
                    wide[pl.ds(start, k2_count, stride=RADIX * 8), :] = block

    def pack(peer, residue):
        at = pl.ds(pl.multiple_of(peer * (RADIX * 8) + residue * 8, 16), 16)
        place = peer * PAIRS + residue // 2
        sent[place] = wide[at, :].astype(jnp.bfloat16)
        return sent.at[place]

    def deliver(residue):
        peer_t, half = residue // times, residue // 2 % 2
        target = (first_got, late_ref)[half].at[tm, chan]

        def remote(peer, source):
            pltpu.make_async_remote_copy(
                source, target, send_sem, recv_sem.at[half],
                device_id=(peer, peer_t), device_id_type=MESH,
            ).start()

        own = pack(chan, residue)

        @pl.when(tm == peer_t)
        def _():
            pltpu.make_async_copy(own, target, own_sem.at[half]).start()

        @pl.when(tm != peer_t)
        def _():
            remote(chan, own)

        def one(step, _):
            peer = lax.rem(chan + step, chans)
            remote(peer, pack(peer, residue))
            return 0

        lax.fori_loop(1, chans, one, 0)

    for place, (q, complete) in enumerate(ORDER):
        transform(q)
        if place == 0:
            pl.semaphore_wait(all_in, line - 1)
        for residue in complete:
            deliver(residue)

    others = sent.at[pl.ds(0, total - 1)]

    def arrived(half):
        pltpu.make_async_copy(sent.at[0], sent.at[0], own_sem.at[half]).wait()
        pltpu.make_async_copy(others, others, recv_sem.at[half]).wait()

    arrived(0)
    for index in range(2):
        parts = channel_gram([first_got[t] for t in range(times)], index, scale)
        for part, value in enumerate(parts):
            early_ref[index, part] = value
    arrived(1)
    both_halves = sent.at[pl.ds(0, 2 * (total - 1))]
    pltpu.make_async_copy(both_halves, both_halves, send_sem).wait()

    @pl.when(tm < times - 1)
    def _():
        pltpu.make_async_copy(tail_out, tail_out, halo_send).wait()


def late_kernel(scale, early_ref, got_ref, vis_ref, late, early_sem, late_sem):
    early_copy = pltpu.make_async_copy(early_ref, vis_ref.at[pl.ds(0, 2)], early_sem)
    early_copy.start()
    copies = []
    for index in range(2):
        parts = channel_gram([got_ref[t] for t in range(got_ref.shape[0])], index, scale)
        for part, value in enumerate(parts):
            late[index, part] = value
        copies.append(
            pltpu.make_async_copy(late.at[index], vis_ref.at[2 + index], late_sem.at[index])
        )
        copies[-1].start()
    early_copy.wait()
    for copy in copies:
        copy.wait()


def body(samples):
    chans = lax.axis_size("chan")
    times = lax.axis_size("tm")
    inputs = samples.shape[0]
    spec = samples.shape[1] // (2 * CH)
    rows = RADIX * inputs
    all_inputs = chans * inputs
    arranged = samples.reshape(inputs, spec, RADIX, LANES).transpose(1, 2, 0, 3)
    arranged = arranged.reshape(spec, rows, LANES)
    weights = jnp.asarray(filter_table(inputs))
    high, low = (jnp.asarray(table) for table in fourier_tables())
    vmem = pl.BlockSpec(memory_space=pltpu.VMEM)
    hbm = pl.BlockSpec(memory_space=pltpu.HBM)
    scale = float(np.float32(1.0 / (NOISE_POWER * spec * times)))
    got_shape = (times, chans, 4 * inputs, LANES)
    vis_shape = (2, 2, all_inputs, all_inputs)
    early, got = pl.pallas_call(
        functools.partial(spectra_kernel, chans, times, inputs, spec, scale),
        out_shape=(
            jax.ShapeDtypeStruct(vis_shape, jnp.float32),
            jax.ShapeDtypeStruct(got_shape, jnp.bfloat16),
        ),
        in_specs=[hbm] * 4,
        out_specs=(vmem, vmem),
        scratch_shapes=[
            pltpu.VMEM((spec, rows, LANES), jnp.int32),
            pltpu.VMEM(weights.shape, jnp.float32),
            pltpu.VMEM(high.shape, jnp.bfloat16),
            pltpu.VMEM(low.shape, jnp.bfloat16),
            pltpu.VMEM((TAPS - 1, rows, LANES), jnp.int32),
            pltpu.VMEM((TAPS - 1, rows, LANES), jnp.bfloat16),
            pltpu.VMEM((TAPS - 1, rows, LANES), jnp.bfloat16),
            pltpu.VMEM((TAPS - 1, rows, LANES), jnp.float32),
            pltpu.VMEM((rows * spec + spec, LANES), jnp.float32),
            pltpu.VMEM((PAIRS, inputs * spec, 2 * LANES), jnp.bfloat16),
            pltpu.VMEM((PAIRS, inputs * spec, 2 * LANES), jnp.bfloat16),
            pltpu.VMEM((chans * PAIRS, 4 * inputs, LANES), jnp.bfloat16),
            pltpu.VMEM(got_shape, jnp.bfloat16),
            pltpu.SemaphoreType.DMA((rows // 8,)),
            pltpu.SemaphoreType.DMA((3,)),
            pltpu.SemaphoreType.DMA,
            pltpu.SemaphoreType.DMA,
            pltpu.SemaphoreType.DMA,
            pltpu.SemaphoreType.DMA,
            pltpu.SemaphoreType.DMA((2,)),
            pltpu.SemaphoreType.DMA((2,)),
            pltpu.SemaphoreType.REGULAR,
        ],
        compiler_params=pltpu.CompilerParams(
            collective_id=0, has_side_effects=True, vmem_limit_bytes=48 << 20
        ),
    )(arranged, *(pltpu.with_memory_space_constraint(v, pltpu.HBM) for v in (weights, high, low)))
    return pl.pallas_call(
        functools.partial(late_kernel, scale),
        out_shape=jax.ShapeDtypeStruct((4, *vis_shape[1:]), jnp.float32),
        in_specs=[vmem, vmem],
        out_specs=hbm,
        scratch_shapes=[
            pltpu.VMEM(vis_shape, jnp.float32),
            pltpu.SemaphoreType.DMA,
            pltpu.SemaphoreType.DMA((2,)),
        ],
        compiler_params=pltpu.CompilerParams(vmem_limit_bytes=40 << 20),
    )(early, got)


def solution(mesh):
    return jax.shard_map(
        body,
        mesh=mesh,
        in_specs=(P("chan", "tm"),),
        out_specs=P(("chan", "tm"), None, None, None),
        check_vma=False,
    )
```
